32 devices in a mesh: panel: 8 (over z, x), cam: 2 (over y), frame: 2 (over core).
Axes of the slice: x: 2, y: 2, z: 4, core: 2. Of those that a mesh axis runs over, the one named last changes fastest.
Arguments:
- front_jc: bfloat16 [1024, 4, 2, 6, 128], P(('panel', 'cam', 'frame')), as said below
- front_jp: bfloat16 [1024, 4, 2, 6, 128], P(('panel', 'cam', 'frame')), as said below
- front_res: bfloat16 [1024, 4, 2, 128], P(('panel', 'cam', 'frame')), may hold values from -96 to 96
- front_corners: int32 [1024, 4, 128], P(('panel', 'cam', 'frame')), may hold values from 0 to 4095
- front_cams: int32 [1024, 4], P(('panel', 'cam', 'frame')), may hold values from 0 to 31
- back_jc: bfloat16 [1024, 4, 2, 6, 128], P(('panel', 'cam', 'frame')), as said below
- back_jp: bfloat16 [1024, 4, 2, 6, 128], P(('panel', 'cam', 'frame')), as said below
- back_res: bfloat16 [1024, 4, 2, 128], P(('panel', 'cam', 'frame')), may hold values from -96 to 96
- back_corners: int32 [1024, 4, 128], P(('panel', 'cam', 'frame')), may hold values from 0 to 4095
- back_cams: int32 [1024, 4], P(('panel', 'cam', 'frame')), may hold values from 0 to 31
- back_match: int32 [1024], P(('panel', 'cam', 'frame')), may hold values from 0 to 31, as said below
- face: int32 [1024], P(('panel', 'cam', 'frame')), may hold values from 0 to 1
- corner_gain: float32 [8192], replicated, may hold values from 0.3 to 3
Outputs:
- cam_step: float32 [6, 128], P(None, 'panel')
- pose_step: float32 [6, 1024], P(None, ('panel', 'cam', 'frame'))
The draws below stay inside these ranges and needn't reach their ends.
Inputs may be any that keep to these rules, and one draw needn't show every extreme that they name: `back_match`: in each aligned block of 32 entries every number appears exactly once. `front_cams`: codes below 8 * 2 name a camera of the storing panel, the others one of the next panel. `front_jc`: camera derivatives of one view. `front_jp`: pose derivatives of one view. `back_jc`: camera derivatives of one view. `back_jp`: pose derivatives of one view.
All inputs are finite; a program needn't handle non-finite values.
Results may differ from the reference program's by a relative error of at most 0.0035.
Values may be sent and summed in bfloat16 or wider, within the bound.
A program may use at most 64 MiB of HBM per device.

```python
import math
import jax
import jax.numpy as jnp
from jax import lax

FRAME_DEV = 32
VIEWS = 4
CORNERS = 128
GRID = 4096
CAM_DEV = 8
ITERS = 4
FRAMES = 1024
CAMERAS = 128
N_PANEL = 8
N_CAM = 2
N_FRAME = 2


def panel_gain(key):
    panel_levels = jnp.exp(jax.random.uniform(jax.random.fold_in(key, 41), (N_PANEL, 1), jnp.float32, -1.0, 1.0))
    return jnp.broadcast_to(panel_levels, (N_PANEL, FRAMES // N_PANEL)).reshape(FRAMES, 1, 1, 1, 1)


def jacobian_pair(key, salt):
    shape = (FRAMES, VIEWS, 2, 6, CORNERS)
    scale = (2.0 * CORNERS) ** (-0.5)
    shared = jax.random.normal(jax.random.fold_in(key, salt), shape, jnp.float32)
    fresh = jax.random.normal(jax.random.fold_in(key, salt + 1), shape, jnp.float32)
    view_scale = jnp.exp(jax.random.uniform(jax.random.fold_in(key, salt + 2), (FRAMES, VIEWS, 1, 1, 1), jnp.float32, -0.35, 0.35))
    total_scale = scale * view_scale * panel_gain(key)
    return (shared * total_scale, (0.8 * shared + 0.6 * fresh) * total_scale)


def draw_front_jc(key, part):
    return jacobian_pair(key, 11)[0].astype(jnp.bfloat16)


def draw_front_jp(key, part):
    return jacobian_pair(key, 11)[1].astype(jnp.bfloat16)


def draw_back_jc(key, part):
    return jacobian_pair(key, 21)[0].astype(jnp.bfloat16)


def draw_back_jp(key, part):
    return jacobian_pair(key, 21)[1].astype(jnp.bfloat16)


def draw_back_match(key, part):
    keys = jax.random.split(jax.random.fold_in(key, 31), FRAMES // FRAME_DEV)
    orders = jax.vmap(lambda single: jax.random.permutation(single, FRAME_DEV))(keys)
    return orders.reshape(FRAMES).astype(jnp.int32)


def with_ends(result, key, least, high):
    extent = result.shape
    index_at = [jax.random.randint(jax.random.fold_in(key, axis), (), 0, extent[axis]) for axis in range(len(extent))]
    result = result.at[tuple(index_at)].set(least)
    longest = extent.index(max(extent))
    index_at[longest] = (index_at[longest] + 1) % extent[longest]
    return result.at[tuple(index_at)].set(high)


def block_levels(own_key, dims, cuts, smallest, largest):
    gain, own = 1.0, jax.random.fold_in(own_key, 6)
    for dim, blocks in cuts:
        draws = jnp.exp(jax.random.uniform(jax.random.fold_in(own, dim), (blocks,), jnp.float32, smallest / len(cuts), largest / len(cuts)))
        gain = gain * jnp.repeat(draws, dims[dim] // blocks).reshape([-1 if axis == dim else 1 for axis in range(len(dims))])
    return gain


def gaussian(stream_key, dims, width, most, cuts=(), held_as=jnp.bfloat16):
    level = block_levels(stream_key, dims, cuts, -0.22, 0.18) if cuts else 1.0
    entries = jax.random.normal(stream_key, dims, jnp.float32) * width * level
    return jnp.minimum(jnp.maximum(entries, -most), most).astype(held_as)


def setup_inputs(seed: int = 0) -> dict:
    streams_of = jax.random.split(jax.random.key(seed), 14)
    return {
        "front_jc": draw_front_jc(jax.random.fold_in(streams_of[13], 71), 0),
        "front_jp": draw_front_jp(jax.random.fold_in(streams_of[13], 71), 0),
        "front_res": gaussian(streams_of[2], (FRAMES, VIEWS, 2, CORNERS), 16.0, 96.0, ((0, 32),)),
        "front_corners": with_ends(jax.random.randint(streams_of[3], (FRAMES, VIEWS, CORNERS), 0, GRID), jax.random.fold_in(streams_of[3], 1), 0, GRID - 1).astype(jnp.int32),
        "front_cams": with_ends(jax.random.randint(streams_of[4], (FRAMES, VIEWS), 0, 2 * CAM_DEV * N_CAM), jax.random.fold_in(streams_of[4], 1), 0, (2 * CAM_DEV * N_CAM) - 1).astype(jnp.int32),
        "back_jc": draw_back_jc(jax.random.fold_in(streams_of[13], 71), 0),
        "back_jp": draw_back_jp(jax.random.fold_in(streams_of[13], 71), 0),
        "back_res": gaussian(streams_of[7], (FRAMES, VIEWS, 2, CORNERS), 16.0, 96.0, ((0, 32),)),
        "back_corners": with_ends(jax.random.randint(streams_of[8], (FRAMES, VIEWS, CORNERS), 0, GRID), jax.random.fold_in(streams_of[8], 1), 0, GRID - 1).astype(jnp.int32),
        "back_cams": with_ends(jax.random.randint(streams_of[9], (FRAMES, VIEWS), 0, 2 * CAM_DEV * N_CAM), jax.random.fold_in(streams_of[9], 1), 0, (2 * CAM_DEV * N_CAM) - 1).astype(jnp.int32),
        "back_match": draw_back_match(jax.random.fold_in(streams_of[13], 71), 0),
        "face": with_ends(jax.random.randint(streams_of[11], (FRAMES,), 0, 2), jax.random.fold_in(streams_of[11], 1), 0, 1).astype(jnp.int32),
        "corner_gain": jnp.clip(jnp.exp(jax.random.uniform(streams_of[12], (2 * GRID,), jnp.float32, math.log(0.3), math.log(3.0))), 0.3, 3.0),
    }


precise = lax.Precision.HIGHEST
damp_pose = 0.1
damp_camera = 0.5


def invert_six(matrix):
    dimension = matrix.shape[-1]
    working = matrix
    inverse = jnp.broadcast_to(jnp.eye(dimension, dtype=matrix.dtype), matrix.shape)
    row_ids = jnp.arange(dimension)[:, None]
    for column in range(dimension):
        pivot = working[..., column:column + 1, column:column + 1]
        row_work = working[..., column:column + 1, :] / pivot
        row_inverse = inverse[..., column:column + 1, :] / pivot
        factor = working[..., :, column:column + 1]
        chosen = row_ids == column
        working = jnp.where(chosen, row_work, working - factor * row_work)
        inverse = jnp.where(chosen, row_inverse, inverse - factor * row_inverse)
    return inverse


def view_grams(jac_cam, jac_pose, residual, corner_ids, face_ids, corner_gain, grid_size):
    weight = jnp.take(corner_gain, face_ids[:, None] * grid_size + corner_ids, axis=0)
    stacked = jnp.concatenate([jac_cam, jac_pose], axis=2)
    weighted = (stacked.astype(jnp.float32) * weight[:, None, None, :]).astype(jnp.bfloat16)
    normal_blocks = jnp.einsum("ncak,ncbk->nab", weighted.astype(jnp.float32), stacked.astype(jnp.float32), precision=precise)
    gradients = jnp.einsum("ncak,nck->na", weighted.astype(jnp.float32), residual.astype(jnp.float32), precision=precise)
    return normal_blocks, gradients


def conjugate(operate, dot_product, right_side, iterations):
    cam_update = jnp.zeros_like(right_side)
    residual = -right_side
    direction = residual
    norm_now = dot_product(residual, residual)
    for iteration in range(iterations):
        image_vec = operate(direction)
        step_size = norm_now / dot_product(direction, image_vec)
        cam_update = cam_update + step_size * direction
        residual = residual - step_size * image_vec
        norm_next = dot_product(residual, residual)
        direction = residual + (norm_next / norm_now) * direction
        norm_now = norm_next
    return cam_update


def reference(front_jc, front_jp, front_res, front_corners, front_cams, back_jc, back_jp, back_res, back_corners, back_cams, back_match, face, corner_gain):
    block_count = FRAMES // FRAME_DEV
    per_panel = CAM_DEV * N_CAM
    group_size = N_CAM * N_FRAME
    per_dev = FRAME_DEV * VIEWS
    frame_ids = jnp.arange(FRAMES, dtype=jnp.int32)
    store_panel = frame_ids // FRAME_DEV // group_size
    home_block = ((store_panel + N_PANEL // 2) % N_PANEL) * group_size + (frame_ids // FRAME_DEV) % group_size
    home_frame = (home_block * FRAME_DEV + back_match).astype(jnp.int32)

    def grams_of(jac_cam, jac_pose, residual, corner_ids, face_ids):
        def per_block(pieces):
            return view_grams(pieces[0], pieces[1], pieces[2], pieces[3], pieces[4], corner_gain, GRID)
        blocks_in = (jac_cam.reshape(block_count, per_dev, 2, 6, CORNERS),
                     jac_pose.reshape(block_count, per_dev, 2, 6, CORNERS),
                     residual.reshape(block_count, per_dev, 2, CORNERS),
                     corner_ids.reshape(block_count, per_dev, CORNERS),
                     jnp.repeat(face_ids, VIEWS).reshape(block_count, per_dev))
        normal_blocks, gradients = lax.map(per_block, blocks_in)
        return normal_blocks.reshape(-1, 12, 12), gradients.reshape(-1, 12)

    gram_front, grad_front = grams_of(front_jc, front_jp, front_res, front_corners, face)
    gram_back, grad_back = grams_of(back_jc, back_jp, back_res, back_corners, 1 - face[home_frame])
    normal_blocks = jnp.concatenate([gram_front, gram_back])
    gradients = jnp.concatenate([grad_front, grad_back])
    cam_block = normal_blocks[:, :6, :6]
    cam_pose = normal_blocks[:, :6, 6:]
    pose_block = normal_blocks[:, 6:, 6:]
    view_frame = jnp.concatenate([jnp.repeat(frame_ids, VIEWS), jnp.repeat(home_frame, VIEWS)])
    view_panel = jnp.concatenate([jnp.repeat(store_panel, VIEWS), jnp.repeat(store_panel, VIEWS)])
    codes = jnp.concatenate([front_cams.reshape(-1), back_cams.reshape(-1)])
    view_cam = (((view_panel + codes // per_panel) % N_PANEL) * per_panel + codes % per_panel).astype(jnp.int32)

    pose_mat = jax.ops.segment_sum(pose_block, view_frame, num_segments=FRAMES) + damp_pose * jnp.eye(6, dtype=jnp.float32)
    pose_inv = invert_six(pose_mat)
    pose_grad = jax.ops.segment_sum(gradients[:, 6:], view_frame, num_segments=FRAMES)

    def couple(x_views):
        return jax.ops.segment_sum(jnp.einsum("nab,na->nb", cam_pose, x_views, precision=precise), view_frame, num_segments=FRAMES)

    def solve_pose(pose_vec):
        return jnp.einsum("fab,fb->fa", pose_inv, pose_vec, precision=precise)

    def spread(pose_vec):
        return jnp.einsum("nab,nb->na", cam_pose, pose_vec[view_frame], precision=precise)

    def operate(vector):
        x_views = vector[view_cam]
        view_terms = jnp.einsum("nab,nb->na", cam_block, x_views, precision=precise) - spread(solve_pose(couple(x_views)))
        return damp_camera * vector + jax.ops.segment_sum(view_terms, view_cam, num_segments=CAMERAS)

    def dot_product(vector_a, vector_b):
        return jnp.sum(vector_a * vector_b)

    right_side = jax.ops.segment_sum(gradients[:, :6] - spread(solve_pose(pose_grad)), view_cam, num_segments=CAMERAS)
    cam_update = conjugate(operate, dot_product, right_side, ITERS)
    pose_update = -solve_pose(pose_grad + couple(cam_update[view_cam]))
    return cam_update.T, pose_update.T
```

```python
import functools

import jax
import jax.numpy as jnp
from jax import lax
from jax.experimental import pallas as pl
from jax.experimental.pallas import tpu as pltpu
from jax.sharding import PartitionSpec as P

CAM_DEV = 8
ITERS = 4
GROUP = 8
LANES = 128
SLOT = 16

precise = lax.Precision.HIGHEST
damp_pose = 0.1
damp_camera = 0.5
MESH = pl.DeviceIdType.MESH


def passed_along(block, axis, distance):
    devices = range(lax.axis_size(axis))
    route = [((i - distance) % len(devices), i) for i in devices]
    return lax.ppermute(block, axis, route)


def invert_six(matrix):
    dimension = matrix.shape[0]
    frames = matrix.shape[2]
    working = [[matrix[i, j] for j in range(dimension)] for i in range(dimension)]
    one, zero = jnp.ones((frames,), matrix.dtype), jnp.zeros((frames,), matrix.dtype)
    inverse = [[one if i == j else zero for j in range(dimension)] for i in range(dimension)]
    for column in range(dimension):
        pivot = 1.0 / working[column][column]
        row_work = [entry * pivot for entry in working[column]]
        row_inverse = [entry * pivot for entry in inverse[column]]
        for row in range(dimension):
            if row == column:
                continue
            factor = working[row][column]
            working[row] = [w - factor * r for w, r in zip(working[row], row_work)]
            inverse[row] = [w - factor * r for w, r in zip(inverse[row], row_inverse)]
        working[column] = row_work
        inverse[column] = row_inverse
    return jnp.stack([jnp.stack(row) for row in inverse])


def gram_kernel(table_rows, fjc, fjp, fres, fcor, fface, bjc, bjp, bres, bcor, bface, gain, front_out, back_out):
    views = fcor.shape[0]
    row_of = lax.broadcasted_iota(jnp.int32, (SLOT, LANES), 0)
    lane_view = lax.broadcasted_iota(jnp.int32, (SLOT, LANES), 1) // SLOT
    sub = lax.broadcasted_iota(jnp.int32, (GROUP, 2, 8, LANES), 2)

    def pad_rows(piece):
        return jnp.concatenate([piece, jnp.zeros(piece.shape[:2] + (2, LANES), piece.dtype)], axis=2)

    for jc, jp, res, cor, face, out in (
        (fjc, fjp, fres, fcor, fface, front_out),
        (bjc, bjp, bres, bcor, bface, back_out),
    ):
        for group in range(views // GROUP):
            rows = pl.ds(group * GROUP, GROUP)
            ids = cor[rows, :]
            low = ids & (LANES - 1)
            high = ids // LANES
            first = jnp.broadcast_to(face[rows, :], (GROUP, LANES)) == 0
            weight = jnp.zeros((GROUP, LANES), jnp.float32)
            for entry in range(table_rows):
                source = jnp.where(
                    first,
                    jnp.broadcast_to(gain[entry : entry + 1, :], (GROUP, LANES)),
                    jnp.broadcast_to(gain[table_rows + entry : table_rows + entry + 1, :], (GROUP, LANES)),
                )
                picked = jnp.take_along_axis(source, low, axis=1, mode="promise_in_bounds")
                weight = jnp.where(high == entry, picked, weight)
            cam = pad_rows(jc[rows].astype(jnp.float32))
            pose = pad_rows(jp[rows].astype(jnp.float32))
            residual = res[rows].astype(jnp.float32)
            pose = jnp.where(sub == 6, residual[:, :, None, :], pose)
            scale = weight[:, None, None, :]
            plain = jnp.concatenate([cam, pose], axis=2)
            scaled = plain * scale
            plain = plain.astype(jnp.bfloat16)
            scaled = scaled.astype(jnp.bfloat16)
            product = jnp.zeros((GROUP * SLOT, LANES), jnp.float32)
            for coord in range(2):
                product = product + lax.dot_general(
                    scaled[:, coord].reshape(GROUP * SLOT, LANES),
                    plain[:, coord].reshape(GROUP * SLOT, LANES),
                    (((1,), (1,)), ((), ())),
                    preferred_element_type=jnp.float32,
                )
            total = jnp.zeros((SLOT, LANES), jnp.float32)
            for view in range(GROUP):
                total = jnp.where(lane_view == view, product[view * SLOT : (view + 1) * SLOT, :], total)
            out[group] = total


def grams(front, back, gain):
    views = front[3].shape[0]
    step = 32
    table_rows = gain.shape[0] // 2 // LANES

    def specs():
        return [
            pl.BlockSpec((step, 2, 6, LANES), lambda i: (i, 0, 0, 0)),
            pl.BlockSpec((step, 2, 6, LANES), lambda i: (i, 0, 0, 0)),
            pl.BlockSpec((step, 2, LANES), lambda i: (i, 0, 0)),
            pl.BlockSpec((step, LANES), lambda i: (i, 0)),
            pl.BlockSpec((step, 1), lambda i: (i, 0)),
        ]

    out = jax.ShapeDtypeStruct((views // GROUP, SLOT, LANES), jnp.float32)
    out_spec = pl.BlockSpec((step // GROUP, SLOT, LANES), lambda i: (i, 0, 0))
    return pl.pallas_call(
        functools.partial(gram_kernel, table_rows),
        grid=(views // step,),
        in_specs=specs() + specs() + [pl.BlockSpec((2 * table_rows, LANES), lambda i: (0, 0))],
        out_specs=(out_spec, out_spec),
        out_shape=(out, out),
        name="grams",
    )(*front, *back, gain.reshape(2 * table_rows, LANES))


def solve_kernel(sizes, per_panel, m_ref, b_ref, out_ref, send, recv, send_sem, recv_sem):
    panels, cams, frames = sizes
    total_devices = panels * cams * frames
    group = cams * frames
    width = max(panels * per_panel, LANES)
    half = panels // 2
    shift = (half - 2) * per_panel
    panel = lax.axis_index("panel")
    me = (panel * cams + lax.axis_index("cam")) * frames + lax.axis_index("frame")

    def coords(device):
        return (device // group, (device // frames) % cams, device % frames)

    barrier = pltpu.get_barrier_semaphore()

    @pl.loop(1, total_devices)
    def _(offset):
        pl.semaphore_signal(barrier, inc=1, device_id=coords((me + offset) % total_devices), device_id_type=MESH)

    pl.semaphore_wait(barrier, total_devices - 1)

    lane = lax.broadcasted_iota(jnp.int32, (8, width), 1)

    def exchange(round_id, row):
        for index in range(3):
            send[round_id, index : index + 1, :] = row[:, index * LANES : (index + 1) * LANES]
            recv[round_id, pl.ds(me, 1), index : index + 1, :] = row[:, index * LANES : (index + 1) * LANES][None]
        send[round_id, 3:4, :] = jnp.zeros((1, LANES), jnp.float32)
        recv[round_id, pl.ds(me, 1), 3:4, :] = jnp.zeros((1, 1, LANES), jnp.float32)

        @pl.loop(1, total_devices)
        def _(offset):
            pltpu.make_async_remote_copy(
                src_ref=send.at[round_id],
                dst_ref=recv.at[round_id, me],
                send_sem=send_sem.at[round_id],
                recv_sem=recv_sem.at[round_id],
                device_id=coords((me + offset) % total_devices),
                device_id_type=MESH,
            ).start()

        others = recv.at[round_id, pl.ds(0, total_devices - 1)]
        pltpu.make_async_copy(others, others, recv_sem.at[round_id]).wait()
        pltpu.make_async_copy(others, others, send_sem.at[round_id]).wait()
        total = jnp.zeros((8, width), jnp.float32)
        for source in range(panels):
            part = recv[round_id, source * group]
            for member in range(1, group):
                part = part + recv[round_id, source * group + member]
            both = jnp.concatenate([part, pltpu.roll(part, LANES // 2, 1)], axis=0)
            if width > LANES:
                both = jnp.concatenate([both, jnp.zeros((8, width - LANES), jnp.float32)], axis=1)
            near = jnp.where(lane < 2 * per_panel, both, 0.0)
            far = jnp.where((lane >= 2 * per_panel) & (lane < 4 * per_panel), both, 0.0)
            if shift % width:
                far = pltpu.roll(far, shift % width, 1)
            placed = near + far
            if source:
                placed = pltpu.roll(placed, source * per_panel, 1)
            total = total + placed
        return total

    def mine(vector):
        turned = pltpu.roll(vector, lax.rem(panels - panel, panels) * per_panel, 1)
        far = pltpu.roll(turned, (width - shift) % width, 1) if shift % width else turned
        return jnp.where(lane < 2 * per_panel, turned, far)[:, :LANES]

    def apply(vector):
        columns = mine(vector).T
        acc = jnp.zeros((8, 3 * LANES), jnp.float32)
        for a in range(6):
            place = a // 2 + 4 * (a % 2)
            column = columns[: 4 * per_panel, place : place + 1]
            scaled = m_ref[a] * column
            acc = acc + jnp.sum(scaled.reshape(4 * per_panel // 8, 8, 3 * LANES), axis=0)
        return jnp.sum(acc, axis=0, keepdims=True)

    def dot(left, right):
        return jnp.sum(jnp.sum(left * right, axis=1, keepdims=True), axis=0, keepdims=True)

    residual = -exchange(0, b_ref[...])
    update = jnp.zeros_like(residual)
    direction = residual
    norm_now = dot(residual, residual)
    for iteration in range(ITERS):
        image = damp_camera * direction + exchange(iteration + 1, apply(direction))
        size = norm_now / dot(direction, image)
        update = update + size * direction
        residual = residual - size * image
        norm_next = dot(residual, residual)
        direction = residual + norm_next / norm_now * direction
        norm_now = norm_next
    out_ref[...] = mine(update)


def solve(sizes, per_panel, m, b):
    total_devices = sizes[0] * sizes[1] * sizes[2]
    return pl.pallas_call(
        functools.partial(solve_kernel, sizes, per_panel),
        in_specs=[pl.BlockSpec(memory_space=pltpu.VMEM)] * 2,
        out_specs=pl.BlockSpec(memory_space=pltpu.VMEM),
        out_shape=jax.ShapeDtypeStruct((8, LANES), jnp.float32),
        scratch_shapes=[
            pltpu.VMEM((ITERS + 1, 4, LANES), jnp.float32),
            pltpu.VMEM((ITERS + 1, total_devices, 4, LANES), jnp.float32),
            pltpu.SemaphoreType.DMA((ITERS + 1,)),
            pltpu.SemaphoreType.DMA((ITERS + 1,)),
        ],
        compiler_params=pltpu.CompilerParams(collective_id=0, has_side_effects=True),
        name="solve",
    )(m, b)


def local(
    sizes,
    front_jc,
    front_jp,
    front_res,
    front_corners,
    front_cams,
    back_jc,
    back_jp,
    back_res,
    back_corners,
    back_cams,
    back_match,
    face,
    corner_gain,
):
    frames = face.shape[0]
    view_count = front_cams.shape[1]
    corners = front_corners.shape[2]
    views = frames * view_count
    half_cycle = sizes[0] // 2
    per_panel = CAM_DEV * sizes[1]
    slots = 4 * per_panel
    frame_ids = jnp.arange(frames, dtype=jnp.int32)

    home_face = passed_along(face, "panel", half_cycle)
    match_table = back_match[:, None] == frame_ids[None, :]
    back_face = 1 - jnp.sum(jnp.where(match_table, home_face[None, :], 0), axis=1)

    def arranged(jc, jp, res, cor, view_face):
        return (
            jc.reshape(views, 2, 6, corners),
            jp.reshape(views, 2, 6, corners),
            res.reshape(views, 2, corners),
            cor.reshape(views, corners),
            jnp.repeat(view_face, view_count)[:, None],
        )

    front_gram, back_gram = grams(
        arranged(front_jc, front_jp, front_res, front_corners, face),
        arranged(back_jc, back_jp, back_res, back_corners, back_face),
        corner_gain,
    )
    moved_gram = passed_along(back_gram, "panel", half_cycle)
    moved_codes, moved_match = passed_along((back_cams, back_match), "panel", half_cycle)

    gram = jnp.concatenate([front_gram, moved_gram]).reshape(2 * views // GROUP, SLOT, GROUP, SLOT)
    gram = gram.transpose(0, 2, 1, 3).reshape(2 * views, SLOT, SLOT)
    cam_block = gram[:, :6, :6]
    cam_pose = gram[:, :6, 8:14]
    pose_block = gram[:, 8:14, 8:14]
    cam_grad = gram[:, :6, 14]
    pose_grads = gram[:, 8:14, 14]

    view_frame = jnp.concatenate([jnp.repeat(frame_ids, view_count), jnp.repeat(moved_match, view_count)])
    frame_table = (view_frame[:, None] == frame_ids[None, :]).astype(jnp.float32)
    view_code = jnp.concatenate([front_cams.reshape(views), moved_codes.reshape(views) + 2 * per_panel])
    cam_table = (view_code[:, None] == jnp.arange(slots, dtype=jnp.int32)[None, :]).astype(jnp.float32)

    pose_mat = jnp.einsum("nab,nf->abf", pose_block, frame_table, precision=precise)
    pose_mat = pose_mat + damp_pose * jnp.eye(6, dtype=jnp.float32)[:, :, None]
    pose_inv = invert_six(pose_mat)
    pose_grad = jnp.einsum("na,nf->af", pose_grads, frame_table, precision=precise)

    spread = (cam_pose[:, :, :, None] * frame_table[:, None, None, :]).reshape(2 * views, 36 * frames)
    coupling = jnp.einsum("nc,nk->ck", cam_table, spread, precision=precise).reshape(slots, 6, 6, frames)
    coupling = coupling.transpose(1, 0, 2, 3)
    solved = jnp.sum(coupling[:, :, :, None, :] * pose_inv[None, None], axis=2)
    flat = coupling.reshape(6 * slots, 6 * frames)
    flat_solved = solved.reshape(6 * slots, 6 * frames)
    diagonal = jnp.einsum("nc,nab->acb", cam_table, cam_block, precision=precise)
    m = -jnp.einsum("ik,jk->ij", flat_solved, flat, precision=precise).reshape(6, slots, 6, slots)
    m = m + diagonal[:, :, :, None] * jnp.eye(slots, dtype=jnp.float32)[None, :, None, :]
    m = m.reshape(6, slots, 6 * slots)
    b = jnp.einsum("nc,na->ac", cam_table, cam_grad, precision=precise).reshape(6 * slots)
    b = b - jnp.einsum("ik,k->i", flat_solved, pose_grad.reshape(6 * frames), precision=precise)

    x = solve(sizes, per_panel, m, b.reshape(1, 6 * slots))
    rows = jnp.stack([x[a // 2 + 4 * (a % 2)] for a in range(6)])
    back_sub = jnp.einsum("ik,i->k", flat_solved, rows[:, :slots].reshape(6 * slots), precision=precise)
    pose_out = -jnp.sum(pose_inv * pose_grad[None], axis=1) - back_sub.reshape(6, frames)
    return rows[:, :per_panel], pose_out


def solution(mesh):
    wide = ("panel", "cam", "frame")
    sizes = tuple(mesh.shape[name] for name in wide)
    in_specs = (
        P(wide, None, None, None, None),
        P(wide, None, None, None, None),
        P(wide, None, None, None),
        P(wide, None, None),
        P(wide, None),
        P(wide, None, None, None, None),
        P(wide, None, None, None, None),
        P(wide, None, None, None),
        P(wide, None, None),
        P(wide, None),
        P(wide),
        P(wide),
        P(),
    )
    out_specs = (P(None, "panel"), P(None, wide))
    return jax.shard_map(
        functools.partial(local, sizes), mesh=mesh, in_specs=in_specs, out_specs=out_specs, check_vma=False
    )
```

```python
import functools

import jax
import jax.numpy as jnp
from jax import lax
from jax.experimental import pallas as pl
from jax.experimental.pallas import tpu as pltpu
from jax.sharding import PartitionSpec as P

CAM_DEV = 8
ITERS = 4
GROUP = 8
LANES = 128
SPAN = 13
WIDE = 256

precise = lax.Precision.HIGHEST
damp_pose = 0.1
damp_camera = 0.5
MESH = pl.DeviceIdType.MESH


def split(values):
    high = values.astype(jnp.bfloat16)
    return high, (values - high.astype(jnp.float32)).astype(jnp.bfloat16)


def mm(left, right, dims):
    return lax.dot_general(left, right, (dims, ((), ())), preferred_element_type=jnp.float32)


ROWS_COLS = ((1,), (0,))
LANES_BOTH = ((1,), (1,))
ROWS_BOTH = ((0,), (0,))


def mm_exact_left(left, right, dims):
    high, low = split(right)
    return mm(left, high, dims) + mm(left, low, dims)


def mm_exact_right(left, right, dims):
    high, low = split(left)
    return mm(high, right, dims) + mm(low, right, dims)


def mm_full(left, right, dims):
    left_high, left_low = split(left)
    right_high, right_low = split(right)
    return mm(left_high, right_high, dims) + (mm(left_high, right_low, dims) + mm(left_low, right_high, dims))


def iota(shape, dim):
    return lax.broadcasted_iota(jnp.int32, shape, dim)


def as_bf16(mask):
    return jnp.where(mask, 1.0, 0.0).astype(jnp.bfloat16)


def invert_six(working):
    dimension = len(working)
    one, zero = jnp.ones_like(working[0][0]), jnp.zeros_like(working[0][0])
    working = [list(row) for row in working]
    inverse = [[one if i == j else zero for j in range(dimension)] for i in range(dimension)]
    for column in range(dimension):
        pivot = 1.0 / working[column][column]
        row_work = [entry * pivot for entry in working[column]]
        row_inverse = [entry * pivot for entry in inverse[column]]
        for row in range(dimension):
            if row == column:
                continue
            factor = working[row][column]
            working[row] = [w - factor * r for w, r in zip(working[row], row_work)]
            inverse[row] = [w - factor * r for w, r in zip(inverse[row], row_inverse)]
        working[column] = row_work
        inverse[column] = row_inverse
    return inverse


def step_kernel(
    sizes, per_panel, frames, view_count,
    fjc, fjp, fres, fcor, fcams, bjc, bjp, bres, bcor, bcams, match, face, gain,
    cam_out, pose_out,
    face_in, match_in, cams_in, gram_send, gram_recv, xbuf, zbuf, vacc, m_ref, ev_ref, send, recv,
    pair_send, pair_recv, send_sem, recv_sem,
):
    panels, cams, frame_devices = sizes
    total_devices = panels * cams * frame_devices
    block = cams * frame_devices
    width = max(panels * per_panel, LANES)
    half = panels // 2
    shift = (half - 2) * per_panel
    slots = 4 * per_panel
    views = frames * view_count
    groups = views // GROUP
    table_rows = gain.shape[0] // 2
    panel = lax.axis_index("panel")
    cam_index = lax.axis_index("cam")
    frame_index = lax.axis_index("frame")
    me = (panel * cams + cam_index) * frame_devices + frame_index

    def coords(device):
        return (device // block, (device // frame_devices) % cams, device % frame_devices)

    barrier = pltpu.get_barrier_semaphore()

    @pl.loop(1, total_devices)
    def _(offset):
        pl.semaphore_signal(barrier, inc=1, device_id=coords((me + offset) % total_devices), device_id_type=MESH)

    partner = (lax.rem(panel + half, panels), cam_index, frame_index)

    def to_partner(index, source, target):
        return pltpu.make_async_remote_copy(
            src_ref=source, dst_ref=target, send_sem=pair_send.at[index], recv_sem=pair_recv.at[index],
            device_id=partner, device_id_type=MESH,
        )

    rows_in = GROUP * 26
    out_row, in_row = iota((rows_in, rows_in), 0), iota((rows_in, rows_in), 1)
    coord, rest = out_row // (SPAN * GROUP), out_row % (SPAN * GROUP)
    quantity, member = rest // GROUP, rest % GROUP
    source_row = jnp.where(
        quantity < 6,
        member * 12 + quantity * 2 + coord,
        jnp.where(quantity < 12, 12 * GROUP + member * 12 + (quantity - 6) * 2 + coord, 24 * GROUP + member * 2 + coord),
    )
    reorder = as_bf16(source_row == in_row)
    same_view = iota((12 * GROUP, SPAN * GROUP), 0) % GROUP == iota((12 * GROUP, SPAN * GROUP), 1) % GROUP
    spread = as_bf16(iota((SPAN * GROUP, WIDE), 0) // GROUP - 6 == iota((SPAN * GROUP, WIDE), 1) // frames)
    view_of = iota((GROUP, frames), 0)
    frame_of = iota((GROUP, frames), 1)

    def column_of(row_ref, group):
        picked = jnp.where(group * (GROUP // view_count) + view_of // view_count == frame_of, row_ref[...], 0)
        return jnp.sum(picked, axis=1, keepdims=True)

    def gram(group, jc, jp, res, cor, face_column):
        ids = cor[pl.ds(group * GROUP, GROUP), :]
        low = ids % LANES
        high = ids // LANES
        first = jnp.broadcast_to(face_column, (GROUP, LANES)) == 0
        weight = jnp.zeros((GROUP, LANES), jnp.float32)
        for entry in range(table_rows):
            source = jnp.where(
                first,
                jnp.broadcast_to(gain[entry : entry + 1, :], (GROUP, LANES)),
                jnp.broadcast_to(gain[table_rows + entry : table_rows + entry + 1, :], (GROUP, LANES)),
            )
            picked = jnp.take_along_axis(source, low, axis=1, mode="promise_in_bounds")
            weight = jnp.where(high == entry, picked, weight)
        stored = jnp.concatenate(
            [
                jc[pl.ds(group * 12 * GROUP, 12 * GROUP), :],
                jp[pl.ds(group * 12 * GROUP, 12 * GROUP), :],
                res[pl.ds(group * 2 * GROUP, 2 * GROUP), :],
            ],
            axis=0,
        )
        ordered = mm(reorder, stored, ROWS_COLS).reshape(2, SPAN, GROUP, LANES)
        product = jnp.zeros((12 * GROUP, SPAN * GROUP), jnp.float32)
        for side in range(2):
            plain = ordered[side]
            scaled = (plain[:12] * weight[None]).reshape(12 * GROUP, LANES).astype(jnp.bfloat16)
            product = product + mm(scaled, plain.reshape(SPAN * GROUP, LANES).astype(jnp.bfloat16), LANES_BOTH)
        return jnp.where(same_view, product, 0.0)

    def keep_camera(group, product):
        for a in range(6):
            zbuf[pl.ds(group * GROUP, GROUP), a * LANES : a * LANES + SPAN * GROUP] = product[a * GROUP : (a + 1) * GROUP]

    lane_frame = iota((GROUP, WIDE), 1) % frames

    def keep_pose(group, wide_product, frame_column):
        chosen = frame_column == lane_frame
        for a in range(6):
            part = wide_product[a * GROUP : (a + 1) * GROUP]
            xbuf[pl.ds(group * GROUP, GROUP), a * WIDE : (a + 1) * WIDE] = jnp.where(chosen, part, 0.0)
        for a in range(6):
            part = wide_product[(6 + a) * GROUP : (7 + a) * GROUP]
            vacc[a] += jnp.where(chosen, part, 0.0)

    zbuf[...] = jnp.zeros_like(zbuf)
    vacc[...] = jnp.zeros_like(vacc)

    def front_group(group):
        product = gram(group, fjc, fjp, fres, fcor, column_of(face, group))
        keep_camera(group, product)
        frame_column = group * (GROUP // view_count) + iota((GROUP, 1), 0) // view_count
        keep_pose(group, mm_exact_right(product, spread, ROWS_COLS), frame_column)

    early = groups // 2

    @pl.loop(0, early)
    def _(group):
        front_group(group)

    pl.semaphore_wait(barrier, total_devices - 1)
    face_copy = to_partner(0, face, face_in)
    match_copy = to_partner(1, match, match_in)
    cams_copy = to_partner(2, bcams, cams_in)
    face_copy.start()
    match_copy.start()
    cams_copy.start()

    @pl.loop(early, groups)
    def _(group):
        front_group(group)

    face_copy.wait()
    gram_send[...] = jnp.zeros_like(gram_send)
    fold_from = iota((SPAN * GROUP, LANES), 0) // GROUP - 6
    fold_to = iota((SPAN * GROUP, LANES), 1)

    @pl.loop(0, groups)
    def _(group):
        match_column = column_of(match, group)
        home_face = jnp.sum(jnp.where(match_column == frame_of, face_in[...], 0), axis=1, keepdims=True)
        product = gram(group, bjc, bjp, bres, bcor, 1 - home_face)
        keep_camera(groups + group, product)
        fold = as_bf16((fold_from >= 0) & (fold_from * groups + group == fold_to))
        gram_send[...] += mm_exact_right(product, fold, ROWS_COLS)

    gram_copy = to_partner(3, gram_send, gram_recv)
    gram_copy.start()

    code_view = iota((views, frames), 0)
    code_frame = iota((views, frames), 1)

    def code_column(code_ref):
        total = jnp.zeros((views, frames), jnp.int32)
        for view in range(view_count):
            hit = (code_view % view_count == view) & (code_view // view_count == code_frame)
            total = jnp.where(hit, code_ref[view : view + 1, :], total)
        return jnp.sum(total, axis=1, keepdims=True)

    slot_of = iota((views, slots), 1)
    front_table = as_bf16(code_column(fcams) == slot_of)
    back_table = as_bf16(code_column(bcams) == slot_of)
    camera = mm_exact_left(jnp.concatenate([front_table, back_table], axis=0), zbuf[...], ROWS_BOTH)
    camera = jnp.concatenate([camera[:, a * LANES : (a + 1) * LANES] for a in range(6)], axis=0)
    total_slots = 6 * slots
    diagonal_spread = as_bf16(iota((LANES, total_slots), 0) // GROUP == iota((LANES, total_slots), 1) // slots)
    diagonal = mm_exact_right(camera, diagonal_spread, ROWS_COLS)
    on_diagonal = iota((total_slots, total_slots), 0) % slots == iota((total_slots, total_slots), 1) % slots
    diagonal = jnp.where(on_diagonal, diagonal, 0.0)
    grad_pick = as_bf16(iota((8, LANES), 1) // GROUP == 12)
    cam_grad = mm_exact_left(grad_pick, camera, LANES_BOTH)[:1]

    match_copy.wait()
    cams_copy.wait()
    gram_copy.wait()
    spread_from = iota((LANES, WIDE), 0)
    spread_to = iota((LANES, WIDE), 1) // frames
    received = split(gram_recv[...])

    @pl.loop(0, groups)
    def _(group):
        place = as_bf16(spread_to * groups + group == spread_from)
        wide_product = mm(received[0], place, ROWS_COLS) + mm(received[1], place, ROWS_COLS)
        keep_pose(groups + group, wide_product, column_of(match_in, group))

    moved_table = as_bf16(code_column(cams_in) + 2 * per_panel == slot_of)
    coupling = mm_exact_left(jnp.concatenate([front_table, moved_table], axis=0), xbuf[...], ROWS_BOTH)
    coupling = jnp.concatenate([coupling[:, a * WIDE : (a + 1) * WIDE] for a in range(6)], axis=0)

    pose_rows = [jnp.sum(vacc[a], axis=0, keepdims=True) for a in range(6)]
    pose_mat = [[pose_rows[a][:, b * frames : (b + 1) * frames] for b in range(7)] for a in range(6)]
    pose_grad = [pose_mat[a][6] for a in range(6)]
    pose_inv = invert_six(
        [[pose_mat[a][b] + damp_pose if a == b else pose_mat[a][b] for b in range(6)] for a in range(6)]
    )
    rest_lanes = jnp.zeros((1, WIDE - 6 * frames), jnp.float32)
    same_frame = iota((frames, WIDE), 0) == iota((frames, WIDE), 1) % frames
    big = []
    for b in range(6):
        row = jnp.concatenate(pose_inv[b] + [rest_lanes], axis=1)
        big.append(jnp.where(same_frame, jnp.broadcast_to(row, (frames, WIDE)), 0.0))
    big.append(jnp.zeros((WIDE - 6 * frames, WIDE), jnp.float32))
    solved = mm_full(coupling, jnp.concatenate(big, axis=0), ROWS_COLS)
    ev_ref[...] = solved
    dense = diagonal - mm_full(solved, coupling, LANES_BOTH)
    m_ref[...] = dense.reshape(6, slots, total_slots)
    grad_row = jnp.broadcast_to(jnp.concatenate(pose_grad + [rest_lanes], axis=1), (8, WIDE))
    right_side = cam_grad - mm_full(grad_row, solved, LANES_BOTH)[:1]
    pose_base = [sum(pose_inv[b][other] * pose_grad[other] for other in range(6)) for b in range(6)]

    lane = iota((8, width), 1)

    def exchange(round_id, row):
        for index in range(3):
            send[round_id, index : index + 1, :] = row[:, index * LANES : (index + 1) * LANES]
            recv[round_id, pl.ds(me, 1), index : index + 1, :] = row[:, index * LANES : (index + 1) * LANES][None]
        send[round_id, 3:4, :] = jnp.zeros((1, LANES), jnp.float32)
        recv[round_id, pl.ds(me, 1), 3:4, :] = jnp.zeros((1, 1, LANES), jnp.float32)

        @pl.loop(1, total_devices)
        def _(offset):
            pltpu.make_async_remote_copy(
                src_ref=send.at[round_id],
                dst_ref=recv.at[round_id, me],
                send_sem=send_sem.at[round_id],
                recv_sem=recv_sem.at[round_id],
                device_id=coords((me + offset) % total_devices),
                device_id_type=MESH,
            ).start()

        others = recv.at[round_id, pl.ds(0, total_devices - 1)]
        pltpu.make_async_copy(others, others, recv_sem.at[round_id]).wait()
        pltpu.make_async_copy(others, others, send_sem.at[round_id]).wait()
        total = jnp.zeros((8, width), jnp.float32)
        for source in range(panels):
            part = recv[round_id, source * block]
            for member in range(1, block):
                part = part + recv[round_id, source * block + member]
            both = jnp.concatenate([part, pltpu.roll(part, LANES // 2, 1)], axis=0)
            if width > LANES:
                both = jnp.concatenate([both, jnp.zeros((8, width - LANES), jnp.float32)], axis=1)
            near = jnp.where(lane < 2 * per_panel, both, 0.0)
            far = jnp.where((lane >= 2 * per_panel) & (lane < 4 * per_panel), both, 0.0)
            if shift % width:
                far = pltpu.roll(far, shift % width, 1)
            placed = near + far
            if source:
                placed = pltpu.roll(placed, source * per_panel, 1)
            total = total + placed
        return total

    def mine(vector):
        turned = pltpu.roll(vector, lax.rem(panels - panel, panels) * per_panel, 1)
        far = pltpu.roll(turned, (width - shift) % width, 1) if shift % width else turned
        return jnp.where(lane < 2 * per_panel, turned, far)[:, :LANES]

    def columns_of(vector):
        columns = mine(vector).T
        return [columns[:slots, a // 2 + 4 * (a % 2) : a // 2 + 4 * (a % 2) + 1] for a in range(6)]

    def apply(vector):
        acc = jnp.zeros((8, total_slots), jnp.float32)
        for a, column in enumerate(columns_of(vector)):
            acc = acc + jnp.sum((m_ref[a] * column).reshape(slots // 8, 8, total_slots), axis=0)
        return jnp.sum(acc, axis=0, keepdims=True)

    def dot(left, right):
        return jnp.sum(jnp.sum(left * right, axis=1, keepdims=True), axis=0, keepdims=True)

    residual = -exchange(0, right_side)
    update = jnp.zeros_like(residual)
    direction = residual
    norm_now = dot(residual, residual)
    for iteration in range(ITERS):
        image = damp_camera * direction + exchange(iteration + 1, apply(direction))
        size = norm_now / dot(direction, image)
        update = update + size * direction
        if iteration + 1 < ITERS:
            residual = residual - size * image
            norm_next = dot(residual, residual)
            direction = residual + norm_next / norm_now * direction
            norm_now = norm_next
    here = mine(update)
    acc = jnp.zeros((8, WIDE), jnp.float32)
    for a, column in enumerate(columns_of(update)):
        place = a // 2 + 4 * (a % 2)
        cam_out[a : a + 1, :] = here[place : place + 1, :per_panel]
        part = ev_ref[a * slots : (a + 1) * slots, :] * column
        acc = acc + jnp.sum(part.reshape(slots // 8, 8, WIDE), axis=0)
    back_row = jnp.sum(acc, axis=0, keepdims=True)
    for b in range(6):
        pose_out[b : b + 1, :] = -(pose_base[b] + back_row[:, b * frames : (b + 1) * frames])


def local(
    sizes,
    front_jc,
    front_jp,
    front_res,
    front_corners,
    front_cams,
    back_jc,
    back_jp,
    back_res,
    back_corners,
    back_cams,
    back_match,
    face,
    corner_gain,
):
    frames = face.shape[0]
    view_count = front_cams.shape[1]
    corners = front_corners.shape[2]
    views = frames * view_count
    per_panel = CAM_DEV * sizes[1]
    slots = 4 * per_panel
    total_devices = sizes[0] * sizes[1] * sizes[2]

    def arranged(jc, jp, res, cor, cams):
        return (
            jc.transpose(0, 1, 3, 2, 4).reshape(views * 12, corners),
            jp.transpose(0, 1, 3, 2, 4).reshape(views * 12, corners),
            res.reshape(views * 2, corners),
            cor.reshape(views, corners),
            cams.T,
        )

    operands = (
        *arranged(front_jc, front_jp, front_res, front_corners, front_cams),
        *arranged(back_jc, back_jp, back_res, back_corners, back_cams),
        back_match.reshape(1, frames),
        face.reshape(1, frames),
        corner_gain.reshape(-1, LANES),
    )
    return pl.pallas_call(
        functools.partial(step_kernel, sizes, per_panel, frames, view_count),
        in_specs=[pl.BlockSpec(memory_space=pltpu.VMEM)] * len(operands),
        out_specs=(pl.BlockSpec(memory_space=pltpu.VMEM),) * 2,
        out_shape=(
            jax.ShapeDtypeStruct((6, per_panel), jnp.float32),
            jax.ShapeDtypeStruct((6, frames), jnp.float32),
        ),
        scratch_shapes=[
            pltpu.VMEM((1, frames), jnp.int32),
            pltpu.VMEM((1, frames), jnp.int32),
            pltpu.VMEM((view_count, frames), jnp.int32),
            pltpu.VMEM((12 * GROUP, LANES), jnp.float32),
            pltpu.VMEM((12 * GROUP, LANES), jnp.float32),
            pltpu.VMEM((2 * views, 6 * WIDE), jnp.float32),
            pltpu.VMEM((2 * views, 6 * LANES), jnp.float32),
            pltpu.VMEM((6, GROUP, WIDE), jnp.float32),
            pltpu.VMEM((6, slots, 6 * slots), jnp.float32),
            pltpu.VMEM((6 * slots, WIDE), jnp.float32),
            pltpu.VMEM((ITERS + 1, 4, LANES), jnp.float32),
            pltpu.VMEM((ITERS + 1, total_devices, 4, LANES), jnp.float32),
            pltpu.SemaphoreType.DMA((4,)),
            pltpu.SemaphoreType.DMA((4,)),
            pltpu.SemaphoreType.DMA((ITERS + 1,)),
            pltpu.SemaphoreType.DMA((ITERS + 1,)),
        ],
        compiler_params=pltpu.CompilerParams(collective_id=0, has_side_effects=True),
        name="gauss_newton",
    )(*operands)


def solution(mesh):
    wide = ("panel", "cam", "frame")
    sizes = tuple(mesh.shape[name] for name in wide)
    in_specs = (
        P(wide, None, None, None, None),
        P(wide, None, None, None, None),
        P(wide, None, None, None),
        P(wide, None, None),
        P(wide, None),
        P(wide, None, None, None, None),
        P(wide, None, None, None, None),
        P(wide, None, None, None),
        P(wide, None, None),
        P(wide, None),
        P(wide),
        P(wide),
        P(),
    )
    out_specs = (P(None, "panel"), P(None, wide))
    return jax.shard_map(
        functools.partial(local, sizes), mesh=mesh, in_specs=in_specs, out_specs=out_specs, check_vma=False
    )
```

```python
import functools

import jax
import jax.numpy as jnp
from jax import lax
from jax.experimental import pallas as pl
from jax.experimental.pallas import tpu as pltpu
from jax.sharding import PartitionSpec as P

CAM_DEV = 8
ITERS = 4
GROUP = 8
LANES = 128
SPAN = 13
WIDE = 256

precise = lax.Precision.HIGHEST
damp_pose = 0.1
damp_camera = 0.5
MESH = pl.DeviceIdType.MESH


def split(values):
    high = values.astype(jnp.bfloat16)
    return high, (values - high.astype(jnp.float32)).astype(jnp.bfloat16)


def mm(left, right, dims):
    return lax.dot_general(left, right, (dims, ((), ())), preferred_element_type=jnp.float32)


ROWS_COLS = ((1,), (0,))
LANES_BOTH = ((1,), (1,))
ROWS_BOTH = ((0,), (0,))


def mm_exact_left(left, right, dims):
    high, low = split(right)
    return mm(left, high, dims) + mm(left, low, dims)


def mm_exact_right(left, right, dims):
    high, low = split(left)
    return mm(high, right, dims) + mm(low, right, dims)


def mm_full(left, right, dims):
    left_high, left_low = split(left)
    right_high, right_low = split(right)
    return mm(left_high, right_high, dims) + (mm(left_high, right_low, dims) + mm(left_low, right_high, dims))


def iota(shape, dim):
    return lax.broadcasted_iota(jnp.int32, shape, dim)


def as_bf16(mask):
    return jnp.where(mask, 1.0, 0.0).astype(jnp.bfloat16)


def invert_six(working):
    dimension = len(working)
    one, zero = jnp.ones_like(working[0][0]), jnp.zeros_like(working[0][0])
    working = [list(row) for row in working]
    inverse = [[one if i == j else zero for j in range(dimension)] for i in range(dimension)]
    for column in range(dimension):
        pivot = 1.0 / working[column][column]
        row_work = [entry * pivot for entry in working[column]]
        row_inverse = [entry * pivot for entry in inverse[column]]
        for row in range(dimension):
            if row == column:
                continue
            factor = working[row][column]
            working[row] = [w - factor * r for w, r in zip(working[row], row_work)]
            inverse[row] = [w - factor * r for w, r in zip(inverse[row], row_inverse)]
        working[column] = row_work
        inverse[column] = row_inverse
    return inverse


def step_kernel(
    sizes, per_panel, frames, view_count,
    fjc, fjp, fres, fcor, fcams, bjc, bjp, bres, bcor, bcams, match, face, gain,
    cam_out, pose_out,
    face_in, match_in, cams_in, gram_send, gram_recv, xbuf, zbuf, vacc, m_ref, ev_ref, send, recv,
    pair_send, pair_recv, send_sem, recv_sem,
):
    panels, cams, frame_devices = sizes
    total_devices = panels * cams * frame_devices
    block = cams * frame_devices
    width = max(panels * per_panel, LANES)
    half = panels // 2
    shift = (half - 2) * per_panel
    slots = 4 * per_panel
    views = frames * view_count
    groups = views // GROUP
    table_rows = gain.shape[0] // 2
    panel = lax.axis_index("panel")
    cam_index = lax.axis_index("cam")
    frame_index = lax.axis_index("frame")
    me = (panel * cams + cam_index) * frame_devices + frame_index

    def coords(device):
        return (device // block, (device // frame_devices) % cams, device % frame_devices)

    upper = panel // half
    other_cam = [(cam_index + turn) % cams for turn in range(cams)]
    other_frame = [(frame_index + turn) % frame_devices for turn in range(frame_devices)]

    barrier = pltpu.get_barrier_semaphore()

    @pl.loop(1, total_devices)
    def _(offset):
        pl.semaphore_signal(barrier, inc=1, device_id=coords((me + offset) % total_devices), device_id_type=MESH)

    partner = (lax.rem(panel + half, panels), cam_index, frame_index)

    def to_partner(index, source, target):
        return pltpu.make_async_remote_copy(
            src_ref=source, dst_ref=target, send_sem=pair_send.at[index], recv_sem=pair_recv.at[index],
            device_id=partner, device_id_type=MESH,
        )

    rows_in = GROUP * 26
    out_row, in_row = iota((rows_in, rows_in), 0), iota((rows_in, rows_in), 1)
    coord, rest = out_row // (SPAN * GROUP), out_row % (SPAN * GROUP)
    quantity, member = rest // GROUP, rest % GROUP
    source_row = jnp.where(
        quantity < 6,
        member * 12 + quantity * 2 + coord,
        jnp.where(quantity < 12, 12 * GROUP + member * 12 + (quantity - 6) * 2 + coord, 24 * GROUP + member * 2 + coord),
    )
    reorder = as_bf16(source_row == in_row)
    same_view = iota((12 * GROUP, SPAN * GROUP), 0) % GROUP == iota((12 * GROUP, SPAN * GROUP), 1) % GROUP
    spread = as_bf16(iota((SPAN * GROUP, WIDE), 0) // GROUP - 6 == iota((SPAN * GROUP, WIDE), 1) // frames)
    view_of = iota((GROUP, frames), 0)
    frame_of = iota((GROUP, frames), 1)

    def column_of(row_ref, group):
        picked = jnp.where(group * (GROUP // view_count) + view_of // view_count == frame_of, row_ref[...], 0)
        return jnp.sum(picked, axis=1, keepdims=True)

    def gram(group, jc, jp, res, cor, face_column):
        ids = cor[pl.ds(group * GROUP, GROUP), :]
        low = ids % LANES
        high = ids // LANES
        first = jnp.broadcast_to(face_column, (GROUP, LANES)) == 0
        weight = jnp.zeros((GROUP, LANES), jnp.float32)
        for entry in range(table_rows):
            source = jnp.where(
                first,
                jnp.broadcast_to(gain[entry : entry + 1, :], (GROUP, LANES)),
                jnp.broadcast_to(gain[table_rows + entry : table_rows + entry + 1, :], (GROUP, LANES)),
            )
            picked = jnp.take_along_axis(source, low, axis=1, mode="promise_in_bounds")
            weight = jnp.where(high == entry, picked, weight)
        stored = jnp.concatenate(
            [
                jc[pl.ds(group * 12 * GROUP, 12 * GROUP), :],
                jp[pl.ds(group * 12 * GROUP, 12 * GROUP), :],
                res[pl.ds(group * 2 * GROUP, 2 * GROUP), :],
            ],
            axis=0,
        )
        ordered = mm(reorder, stored, ROWS_COLS).reshape(2, SPAN, GROUP, LANES)
        product = jnp.zeros((12 * GROUP, SPAN * GROUP), jnp.float32)
        for side in range(2):
            plain = ordered[side]
            scaled = (plain[:12] * weight[None]).reshape(12 * GROUP, LANES).astype(jnp.bfloat16)
            product = product + mm(scaled, plain.reshape(SPAN * GROUP, LANES).astype(jnp.bfloat16), LANES_BOTH)
        return jnp.where(same_view, product, 0.0)

    def keep_camera(group, product):
        for a in range(6):
            zbuf[pl.ds(group * GROUP, GROUP), a * LANES : a * LANES + SPAN * GROUP] = product[a * GROUP : (a + 1) * GROUP]

    lane_frame = iota((GROUP, WIDE), 1) % frames

    def keep_pose(group, wide_product, frame_column):
        chosen = frame_column == lane_frame
        for a in range(6):
            part = wide_product[a * GROUP : (a + 1) * GROUP]
            xbuf[pl.ds(group * GROUP, GROUP), a * WIDE : (a + 1) * WIDE] = jnp.where(chosen, part, 0.0)
        for a in range(6):
            part = wide_product[(6 + a) * GROUP : (7 + a) * GROUP]
            vacc[a] += jnp.where(chosen, part, 0.0)

    zbuf[...] = jnp.zeros_like(zbuf)
    vacc[...] = jnp.zeros_like(vacc)

    def front_group(group):
        product = gram(group, fjc, fjp, fres, fcor, column_of(face, group))
        keep_camera(group, product)
        frame_column = group * (GROUP // view_count) + iota((GROUP, 1), 0) // view_count
        keep_pose(group, mm_exact_right(product, spread, ROWS_COLS), frame_column)

    early = groups // 2

    @pl.loop(0, early, unroll=8)
    def _(group):
        front_group(group)

    pl.semaphore_wait(barrier, total_devices - 1)
    face_copy = to_partner(0, face, face_in)
    match_copy = to_partner(1, match, match_in)
    cams_copy = to_partner(2, bcams, cams_in)
    face_copy.start()
    match_copy.start()
    cams_copy.start()

    @pl.loop(early, groups, unroll=8)
    def _(group):
        front_group(group)

    face_copy.wait()
    gram_send[...] = jnp.zeros_like(gram_send)
    fold_from = iota((SPAN * GROUP, LANES), 0) // GROUP - 6
    fold_to = iota((SPAN * GROUP, LANES), 1)

    @pl.loop(0, groups, unroll=8)
    def _(group):
        match_column = column_of(match, group)
        home_face = jnp.sum(jnp.where(match_column == frame_of, face_in[...], 0), axis=1, keepdims=True)
        product = gram(group, bjc, bjp, bres, bcor, 1 - home_face)
        keep_camera(groups + group, product)
        fold = as_bf16((fold_from >= 0) & (fold_from * groups + group == fold_to))
        gram_send[...] += mm_exact_right(product, fold, ROWS_COLS)

    gram_copy = to_partner(3, gram_send, gram_recv)
    gram_copy.start()

    code_view = iota((views, frames), 0)
    code_frame = iota((views, frames), 1)

    def code_column(code_ref):
        total = jnp.zeros((views, frames), jnp.int32)
        for view in range(view_count):
            hit = (code_view % view_count == view) & (code_view // view_count == code_frame)
            total = jnp.where(hit, code_ref[view : view + 1, :], total)
        return jnp.sum(total, axis=1, keepdims=True)

    slot_of = iota((views, slots), 1)
    front_table = as_bf16(code_column(fcams) == slot_of)
    back_table = as_bf16(code_column(bcams) == slot_of)
    camera = mm_exact_left(jnp.concatenate([front_table, back_table], axis=0), zbuf[...], ROWS_BOTH)
    camera = jnp.concatenate([camera[:, a * LANES : (a + 1) * LANES] for a in range(6)], axis=0)
    total_slots = 6 * slots
    diagonal_spread = as_bf16(iota((LANES, total_slots), 0) // GROUP == iota((LANES, total_slots), 1) // slots)
    diagonal = mm_exact_right(camera, diagonal_spread, ROWS_COLS)
    on_diagonal = iota((total_slots, total_slots), 0) % slots == iota((total_slots, total_slots), 1) % slots
    diagonal = jnp.where(on_diagonal, diagonal, 0.0)
    grad_pick = as_bf16(iota((8, LANES), 1) // GROUP == 12)
    cam_grad = mm_exact_left(grad_pick, camera, LANES_BOTH)[:1]

    match_copy.wait()
    cams_copy.wait()
    gram_copy.wait()
    spread_from = iota((LANES, WIDE), 0)
    spread_to = iota((LANES, WIDE), 1) // frames
    received = split(gram_recv[...])

    @pl.loop(0, groups, unroll=8)
    def _(group):
        place = as_bf16(spread_to * groups + group == spread_from)
        wide_product = mm(received[0], place, ROWS_COLS) + mm(received[1], place, ROWS_COLS)
        keep_pose(groups + group, wide_product, column_of(match_in, group))

    moved_table = as_bf16(code_column(cams_in) + 2 * per_panel == slot_of)
    coupling = mm_exact_left(jnp.concatenate([front_table, moved_table], axis=0), xbuf[...], ROWS_BOTH)
    coupling = jnp.concatenate([coupling[:, a * WIDE : (a + 1) * WIDE] for a in range(6)], axis=0)

    pose_rows = [jnp.sum(vacc[a], axis=0, keepdims=True) for a in range(6)]
    pose_mat = [[pose_rows[a][:, b * frames : (b + 1) * frames] for b in range(7)] for a in range(6)]
    pose_grad = [pose_mat[a][6] for a in range(6)]
    pose_inv = invert_six(
        [[pose_mat[a][b] + damp_pose if a == b else pose_mat[a][b] for b in range(6)] for a in range(6)]
    )
    rest_lanes = jnp.zeros((1, WIDE - 6 * frames), jnp.float32)
    same_frame = iota((frames, WIDE), 0) == iota((frames, WIDE), 1) % frames
    big = []
    for b in range(6):
        row = jnp.concatenate(pose_inv[b] + [rest_lanes], axis=1)
        big.append(jnp.where(same_frame, jnp.broadcast_to(row, (frames, WIDE)), 0.0))
    big.append(jnp.zeros((WIDE - 6 * frames, WIDE), jnp.float32))
    solved = mm_full(coupling, jnp.concatenate(big, axis=0), ROWS_COLS)
    ev_ref[...] = solved
    dense = diagonal - mm_full(solved, coupling, LANES_BOTH)
    m_ref[...] = dense.reshape(6, slots, total_slots)
    grad_row = jnp.broadcast_to(jnp.concatenate(pose_grad + [rest_lanes], axis=1), (8, WIDE))
    right_side = cam_grad - mm_full(grad_row, solved, LANES_BOTH)[:1]
    pose_base = [sum(pose_inv[b][other] * pose_grad[other] for other in range(6)) for b in range(6)]

    lane = iota((8, width), 1)

    def exchange(round_id, row):
        for index in range(3):
            send[round_id, index : index + 1, :] = row[:, index * LANES : (index + 1) * LANES]
            recv[round_id, pl.ds(me, 1), index : index + 1, :] = row[:, index * LANES : (index + 1) * LANES][None]

        def send_to(device):
            pltpu.make_async_remote_copy(
                src_ref=send.at[round_id],
                dst_ref=recv.at[round_id, me],
                send_sem=send_sem.at[round_id],
                recv_sem=recv_sem.at[round_id],
                device_id=device,
                device_id_type=MESH,
            ).start()

        def send_panel(order):
            target = upper * order + (1 - upper) * (panels - 1 - order)
            for turn in range(1, block):
                send_to((target, other_cam[turn // frame_devices], other_frame[turn % frame_devices]))

            @pl.when(target != panel)
            def _():
                send_to((target, cam_index, frame_index))

        if panels <= 8:
            for order in range(panels):
                send_panel(order)
        else:
            pl.loop(0, panels)(send_panel)

        others = recv.at[round_id, pl.ds(0, total_devices - 1)]
        pltpu.make_async_copy(others, others, recv_sem.at[round_id]).wait()
        pltpu.make_async_copy(others, others, send_sem.at[round_id]).wait()
        total = jnp.zeros((8, width), jnp.float32)
        for source in range(panels):
            part = recv[round_id, source * block]
            for member in range(1, block):
                part = part + recv[round_id, source * block + member]
            part = jnp.concatenate([part, jnp.zeros((1, LANES), jnp.float32)], axis=0)
            both = jnp.concatenate([part, pltpu.roll(part, LANES // 2, 1)], axis=0)
            if width > LANES:
                both = jnp.concatenate([both, jnp.zeros((8, width - LANES), jnp.float32)], axis=1)
            near = jnp.where(lane < 2 * per_panel, both, 0.0)
            far = jnp.where((lane >= 2 * per_panel) & (lane < 4 * per_panel), both, 0.0)
            if shift % width:
                far = pltpu.roll(far, shift % width, 1)
            placed = near + far
            if source:
                placed = pltpu.roll(placed, source * per_panel, 1)
            total = total + placed
        return total

    def mine(vector):
        turned = pltpu.roll(vector, lax.rem(panels - panel, panels) * per_panel, 1)
        far = pltpu.roll(turned, (width - shift) % width, 1) if shift % width else turned
        return jnp.where(lane < 2 * per_panel, turned, far)[:, :LANES]

    def columns_of(vector):
        columns = mine(vector).T
        return [columns[:slots, a // 2 + 4 * (a % 2) : a // 2 + 4 * (a % 2) + 1] for a in range(6)]

    def apply(vector):
        acc = jnp.zeros((8, total_slots), jnp.float32)
        for a, column in enumerate(columns_of(vector)):
            acc = acc + jnp.sum((m_ref[a] * column).reshape(slots // 8, 8, total_slots), axis=0)
        return jnp.sum(acc, axis=0, keepdims=True)

    def dot(left, right):
        return jnp.sum(jnp.sum(left * right, axis=1, keepdims=True), axis=0, keepdims=True)

    residual = -exchange(0, right_side)
    update = jnp.zeros_like(residual)
    direction = residual
    norm_now = dot(residual, residual)
    for iteration in range(ITERS):
        image = damp_camera * direction + exchange(iteration + 1, apply(direction))
        size = norm_now / dot(direction, image)
        update = update + size * direction
        if iteration + 1 < ITERS:
            residual = residual - size * image
            norm_next = dot(residual, residual)
            direction = residual + norm_next / norm_now * direction
            norm_now = norm_next
    here = mine(update)
    acc = jnp.zeros((8, WIDE), jnp.float32)
    for a, column in enumerate(columns_of(update)):
        place = a // 2 + 4 * (a % 2)
        cam_out[a : a + 1, :] = here[place : place + 1, :per_panel]
        part = ev_ref[a * slots : (a + 1) * slots, :] * column
        acc = acc + jnp.sum(part.reshape(slots // 8, 8, WIDE), axis=0)
    back_row = jnp.sum(acc, axis=0, keepdims=True)
    for b in range(6):
        pose_out[b : b + 1, :] = -(pose_base[b] + back_row[:, b * frames : (b + 1) * frames])


def local(
    sizes,
    front_jc,
    front_jp,
    front_res,
    front_corners,
    front_cams,
    back_jc,
    back_jp,
    back_res,
    back_corners,
    back_cams,
    back_match,
    face,
    corner_gain,
):
    frames = face.shape[0]
    view_count = front_cams.shape[1]
    corners = front_corners.shape[2]
    views = frames * view_count
    per_panel = CAM_DEV * sizes[1]
    slots = 4 * per_panel
    total_devices = sizes[0] * sizes[1] * sizes[2]

    def arranged(jc, jp, res, cor, cams):
        return (
            jc.transpose(0, 1, 3, 2, 4).reshape(views * 12, corners),
            jp.transpose(0, 1, 3, 2, 4).reshape(views * 12, corners),
            res.reshape(views * 2, corners),
            cor.reshape(views, corners),
            cams.T,
        )

    operands = (
        *arranged(front_jc, front_jp, front_res, front_corners, front_cams),
        *arranged(back_jc, back_jp, back_res, back_corners, back_cams),
        back_match.reshape(1, frames),
        face.reshape(1, frames),
        corner_gain.reshape(-1, LANES),
    )
    return pl.pallas_call(
        functools.partial(step_kernel, sizes, per_panel, frames, view_count),
        in_specs=[pl.BlockSpec(memory_space=pltpu.VMEM)] * len(operands),
        out_specs=(pl.BlockSpec(memory_space=pltpu.VMEM),) * 2,
        out_shape=(
            jax.ShapeDtypeStruct((6, per_panel), jnp.float32),
            jax.ShapeDtypeStruct((6, frames), jnp.float32),
        ),
        scratch_shapes=[
            pltpu.VMEM((1, frames), jnp.int32),
            pltpu.VMEM((1, frames), jnp.int32),
            pltpu.VMEM((view_count, frames), jnp.int32),
            pltpu.VMEM((12 * GROUP, LANES), jnp.float32),
            pltpu.VMEM((12 * GROUP, LANES), jnp.float32),
            pltpu.VMEM((2 * views, 6 * WIDE), jnp.float32),
            pltpu.VMEM((2 * views, 6 * LANES), jnp.float32),
            pltpu.VMEM((6, GROUP, WIDE), jnp.float32),
            pltpu.VMEM((6, slots, 6 * slots), jnp.float32),
            pltpu.VMEM((6 * slots, WIDE), jnp.float32),
            pltpu.VMEM((ITERS + 1, 3, LANES), jnp.float32),
            pltpu.VMEM((ITERS + 1, total_devices, 3, LANES), jnp.float32),
            pltpu.SemaphoreType.DMA((4,)),
            pltpu.SemaphoreType.DMA((4,)),
            pltpu.SemaphoreType.DMA((ITERS + 1,)),
            pltpu.SemaphoreType.DMA((ITERS + 1,)),
        ],
        compiler_params=pltpu.CompilerParams(collective_id=0, has_side_effects=True),
        name="gauss_newton",
    )(*operands)


def solution(mesh):
    wide = ("panel", "cam", "frame")
    sizes = tuple(mesh.shape[name] for name in wide)
    in_specs = (
        P(wide, None, None, None, None),
        P(wide, None, None, None, None),
        P(wide, None, None, None),
        P(wide, None, None),
        P(wide, None),
        P(wide, None, None, None, None),
        P(wide, None, None, None, None),
        P(wide, None, None, None),
        P(wide, None, None),
        P(wide, None),
        P(wide),
        P(wide),
        P(),
    )
    out_specs = (P(None, "panel"), P(None, wide))
    return jax.shard_map(
        functools.partial(local, sizes), mesh=mesh, in_specs=in_specs, out_specs=out_specs, check_vma=False
    )
```
